256 devices in a mesh: head: 4 (over z_hi, core), inner: 16 (over z_lo, x), outer: 4 (over y).
Axes of the slice: x: 4, y: 4, z: 8 (z_hi: 2, z_lo: 4; z = z_hi * 4 + z_lo), core: 2. Of those that a mesh axis runs over, the one named last changes fastest.
Arguments:
- query_states: bfloat16 [8192, 8192], P('outer', 'inner'), may hold values from -110 to 110
- context_hidden_states: bfloat16 [16384, 8192], P(('inner', 'outer'), 'head'), may hold values from -6 to 6
- key_segments: int32 [128], P(('inner', 'outer')), may hold values from 0 to 6, as said below
- query_segments: int32 [8192], P('outer'), may hold values from 1 to 6, as said below
- w_query: bfloat16 [8192, 4096], P('inner', 'head'), may hold values from -0.1875 to 0.1875
- key_value_weight: bfloat16 [8192, 4, 256], P('head'), may hold values from -0.0625 to 0.0625
- w_output: bfloat16 [4096, 4, 2048], P('head', None, 'inner'), may hold values from -0.09375 to 0.09375
Outputs:
- mixed: bfloat16 [8192, 8192], P('outer', ('head', 'inner'))
The draws below stay inside these ranges and needn't reach their ends.
Inputs may be any that keep to these rules, and one draw needn't show every extreme that they name: `key_segments`: block 0 is repository code (0) and the last block has segment 6. `query_segments`: the first query token has span 1 and the last has span 6.
All inputs are finite; a program needn't handle non-finite values.
Results may differ from the reference program's by a relative error of at most 0.0173.
The reference program's roundings to bfloat16 on the way (of `queries` and `attended`) count: a program that leaves them out, or rounds other values in their place, can miss the bound.
Values may be sent and summed in bfloat16 or wider, within the bound.
A program may use at most 128 MiB of HBM per device.

```python
import math
import jax
import jax.numpy as jnp
from jax import lax

MODEL_WIDTH = 8192
HEAD_SIZE = 128
QUERY_HEADS = 32
KEY_VALUE_HEADS = 4
KBLK = 128
QWIN = 512
NSEG = 6
CONTEXT_TOKENS = 16384
QTOK = 8192
QDIM = 4096
N_HEAD = 4


def draw_query_states(key, part):
    base = jax.random.normal(jax.random.fold_in(key, 13), (QTOK, MODEL_WIDTH), jnp.float32)
    return jnp.clip(base, -6.0, 6.0).astype(jnp.bfloat16)


def draw_key_segments(key, part):
    count = CONTEXT_TOKENS // KBLK
    raw = jax.random.randint(jax.random.fold_in(key, 21), (count,), 0, NSEG + 1)
    place = jnp.arange(count)
    raw = jnp.where(place == 0, 0, raw)
    raw = jnp.where(place == count - 1, NSEG, raw)
    return raw.astype(jnp.int32)


def draw_query_segments(key, part):
    raw = jax.random.randint(jax.random.fold_in(key, 31), (QTOK,), 1, NSEG + 1)
    place = jnp.arange(QTOK)
    raw = jnp.where(place == 0, 1, raw)
    raw = jnp.where(place == QTOK - 1, NSEG, raw)
    return raw.astype(jnp.int32)


def steps_of(stream_key, extent, shards, low, largest):
    gain = 1.0
    for position, shards_of in shards:
        steps = jax.random.uniform(jax.random.fold_in(jax.random.fold_in(stream_key, 6), position), (shards_of,), jnp.float32, low / len(shards), largest / len(shards))
        gain = gain * jnp.repeat(jnp.exp(steps), extent[position] // shards_of).reshape((-1,) + (1,) * (len(extent) - 1 - position))
    return gain


def normal_values(own_key, dims, scale, reach, split=(), kind=jnp.bfloat16):
    drawn = jax.random.normal(own_key, dims, jnp.float32) * scale
    if len(split) > 0:
        drawn = steps_of(own_key, dims, split, -0.22, 0.18) * drawn
    return jnp.clip(drawn, min=-reach, max=reach).astype(kind)


def setup_inputs(seed: int = 0) -> dict:
    key_list = jax.random.split(jax.random.key(seed), 8)
    return {
        "query_states": draw_query_states(jax.random.fold_in(key_list[7], 71), 0),
        "context_hidden_states": normal_values(key_list[1], (CONTEXT_TOKENS, MODEL_WIDTH), 1.0, 6.0, ((0, 64), (1, 4))),
        "key_segments": draw_key_segments(jax.random.fold_in(key_list[7], 71), 0),
        "query_segments": draw_query_segments(jax.random.fold_in(key_list[7], 71), 0),
        "w_query": normal_values(key_list[4], (MODEL_WIDTH, QDIM), (MODEL_WIDTH // 9) ** -0.5, 0.1875, ((0, 16), (1, 4))),
        "key_value_weight": normal_values(key_list[5], (MODEL_WIDTH, KEY_VALUE_HEADS, 2 * HEAD_SIZE), MODEL_WIDTH ** -0.5, 0.0625, ((0, 4),)),
        "w_output": normal_values(key_list[6], (QDIM, N_HEAD, MODEL_WIDTH // N_HEAD), QDIM ** -0.5, 0.09375, ((0, 4), (2, 16))),
    }


ROPE_BASE = 1000000.0
NEG_FILL = -1e+30

def rotate(vectors, positions):
    half = HEAD_SIZE // 2
    freqs = jnp.power(ROPE_BASE, -(jnp.arange(half).astype(jnp.float32) * 2.0 / HEAD_SIZE))
    angles = positions[:, None] * freqs[None, :]
    cosine = jnp.cos(angles)[:, None, :]
    sine = jnp.sin(angles)[:, None, :]
    lower = vectors[..., :half]
    upper = vectors[..., half:]
    return jnp.concatenate([lower * cosine - upper * sine, upper * cosine + lower * sine], axis=-1)

def reference(query_states, context_hidden_states, key_segments, query_segments, w_query, key_value_weight, w_output):
    projected_q = jnp.dot(query_states, w_query, preferred_element_type=jnp.float32).reshape(QTOK, QUERY_HEADS, HEAD_SIZE)
    query_pos = (CONTEXT_TOKENS + jnp.arange(QTOK) % QWIN).astype(jnp.float32)
    queries = rotate(projected_q, query_pos).astype(jnp.bfloat16)
    projected_context = jnp.dot(context_hidden_states, key_value_weight.reshape(MODEL_WIDTH, KEY_VALUE_HEADS * 2 * HEAD_SIZE), preferred_element_type=jnp.float32)
    projected_context = projected_context.reshape(CONTEXT_TOKENS, KEY_VALUE_HEADS, 2 * HEAD_SIZE)
    key_pos = jnp.arange(CONTEXT_TOKENS).astype(jnp.float32)
    keys = rotate(projected_context[:, :, :HEAD_SIZE], key_pos).astype(jnp.bfloat16)
    values = projected_context[:, :, HEAD_SIZE:].astype(jnp.bfloat16)
    keys_wide = keys.astype(jnp.float32)
    values_wide = values.astype(jnp.float32)
    key_tags = jnp.repeat(key_segments, KBLK)
    head_repeat_count = QUERY_HEADS // KEY_VALUE_HEADS
    scale = 1.0 / math.sqrt(HEAD_SIZE)
    block_row_span = math.gcd(QTOK, 128)
    blocks = QTOK // block_row_span

    def one_block(members):
        query_row_block, segment_block = members
        grouped_heads = query_row_block.astype(jnp.float32).reshape(block_row_span, KEY_VALUE_HEADS, head_repeat_count, HEAD_SIZE)
        scores = jnp.einsum('bgph,ngh->bgpn', grouped_heads, keys_wide) * scale
        allowed = (key_tags[None, :] == 0) | (key_tags[None, :] == segment_block[:, None])
        allowed = allowed[:, None, None, :]
        highest = lax.optimization_barrier(jnp.max(jnp.where(allowed, scores, NEG_FILL), axis=-1, keepdims=True))
        weights = jnp.where(allowed, jnp.exp(scores - highest), 0.0)
        denominator = lax.optimization_barrier(jnp.sum(weights, axis=-1))
        rounded = lax.optimization_barrier(weights.astype(jnp.bfloat16)).astype(jnp.float32)
        summed = jnp.einsum('bgpn,ngh->bgph', rounded, values_wide)
        return (summed / denominator[..., None]).reshape(block_row_span, QDIM).astype(jnp.bfloat16)
    attended = lax.map(one_block, (queries.reshape(blocks, block_row_span, QUERY_HEADS, HEAD_SIZE), query_segments.reshape(blocks, block_row_span)))
    attended = attended.reshape(QTOK, QDIM)
    result = jnp.dot(attended, w_output.reshape(QDIM, MODEL_WIDTH), preferred_element_type=jnp.float32)
    return result.astype(jnp.bfloat16)
```

```python
import math

import jax
import jax.numpy as jnp
from jax import lax
from jax.experimental import pallas as pl
from jax.experimental.pallas import tpu as pltpu
from jax.sharding import PartitionSpec as P

HEAD_SIZE = 128
KBLK = 128
QWIN = 512
ROPE_BASE = 1000000.0
PENALTY = -1e30
SCALE2 = math.log2(math.e) / math.sqrt(HEAD_SIZE)


def rotate(vectors, positions):
    half = HEAD_SIZE // 2
    freqs = jnp.power(ROPE_BASE, -(jnp.arange(half).astype(jnp.float32) * 2.0 / HEAD_SIZE))
    angles = positions[:, None] * freqs[None, :]
    cosine = jnp.cos(angles)[:, None, :]
    sine = jnp.sin(angles)[:, None, :]
    lower = vectors[..., :half]
    upper = vectors[..., half:]
    return jnp.concatenate([lower * cosine - upper * sine, upper * cosine + lower * sine], axis=-1)


def attention_kernel(heads, tile, chunk, q_ref, hot_ref, ka_ref, va_ref, o_ref, lse_ref, s_ref, m_ref):
    tokens = q_ref.shape[0]
    keys = ka_ref.shape[0]
    halves = tokens // tile
    steps = heads * halves
    chunks = keys // chunk

    def rows_of(t):
        return pl.ds(pl.multiple_of(lax.rem(t, halves) * tile, tile), tile)

    def cols_of(t):
        return pl.ds(pl.multiple_of(lax.div(t, halves) * HEAD_SIZE, HEAD_SIZE), HEAD_SIZE)

    def score(t, slot, c):
        qa = jnp.concatenate([q_ref[rows_of(t), cols_of(t)], hot_ref[rows_of(t), :]], axis=-1)
        s = lax.dot_general(
            qa, ka_ref[c * chunk : (c + 1) * chunk, :],
            (((1,), (1,)), ((), ())), preferred_element_type=jnp.float32,
        )
        s_ref[slot, :, c * chunk : (c + 1) * chunk] = s
        best = s[:, :HEAD_SIZE]
        for j in range(1, chunk // HEAD_SIZE):
            best = jnp.maximum(best, s[:, j * HEAD_SIZE : (j + 1) * HEAD_SIZE])
        return best

    def top_of(bests):
        best = bests[0]
        for b in bests[1:]:
            best = jnp.maximum(best, b)
        return jnp.broadcast_to(jnp.max(best, axis=-1, keepdims=True) * SCALE2, (tile, HEAD_SIZE))

    m_ref[0] = top_of([score(0, 0, c) for c in range(chunks)])
    lane = lax.broadcasted_iota(jnp.int32, (tile, HEAD_SIZE), 1)

    def body(t, carry):
        slot = lax.rem(t, 2)
        nxt = jnp.minimum(t + 1, steps - 1)
        m = m_ref[slot]
        acc = jnp.zeros((tile, 2 * HEAD_SIZE), jnp.float32)
        bests = []
        mw = jnp.concatenate([m] * (chunk // HEAD_SIZE), axis=-1)
        for c in range(chunks):
            p = jnp.exp2(s_ref[slot, :, c * chunk : (c + 1) * chunk] * SCALE2 - mw)
            bests.append(score(nxt, 1 - slot, c))
            acc += jnp.dot(p.astype(jnp.bfloat16), va_ref[c * chunk : (c + 1) * chunk, :], preferred_element_type=jnp.float32)
        m_ref[1 - slot] = top_of(bests)
        total = acc[:, HEAD_SIZE:]
        o_ref[rows_of(t), cols_of(t)] = (acc[:, :HEAD_SIZE] / total).astype(jnp.bfloat16)
        lse = m + jnp.log2(total)
        old = lse_ref[rows_of(t), :]
        lse_ref[rows_of(t), :] = jnp.where(lane == lax.div(t, halves), lse, old)
        return carry

    lse_ref[...] = jnp.zeros_like(lse_ref)
    lax.fori_loop(0, steps, body, 0)


def attention(q, hot, ka, va, heads, tile=256, chunk=512):
    tokens = q.shape[0]
    keys = ka.shape[0]
    return pl.pallas_call(
        lambda *refs: attention_kernel(heads, tile, chunk, *refs),
        out_shape=(
            jax.ShapeDtypeStruct(q.shape, jnp.bfloat16),
            jax.ShapeDtypeStruct((tokens, HEAD_SIZE), jnp.float32),
        ),
        in_specs=[pl.BlockSpec(memory_space=pltpu.VMEM)] * 4,
        out_specs=(pl.BlockSpec(memory_space=pltpu.VMEM),) * 2,
        scratch_shapes=[
            pltpu.VMEM((2, tile, keys), jnp.float32),
            pltpu.VMEM((2, tile, HEAD_SIZE), jnp.float32),
        ],
        compiler_params=pltpu.CompilerParams(vmem_limit_bytes=48 * 1024 * 1024),
        name="attention",
    )(q, hot, ka, va)


def penalties(tags, rows):
    lane = jnp.arange(HEAD_SIZE, dtype=jnp.int32)
    row = jnp.where((tags[:, None] == 0) | (tags[:, None] == lane[None, :]), 0.0, PENALTY)
    return jnp.repeat(row.astype(jnp.bfloat16), rows, axis=0)


def on_device(
    query_states,
    context_hidden_states,
    key_segments,
    query_segments,
    w_query,
    key_value_weight,
    w_output,
):
    head_count = lax.axis_size("head")
    inner_count = lax.axis_size("inner")
    outer_count = lax.axis_size("outer")
    inner_at = lax.axis_index("inner")
    outer_at = lax.axis_index("outer")
    query_rows = query_states.shape[0] // inner_count
    query_cols = w_query.shape[1]
    heads = query_cols // HEAD_SIZE
    context_rows = context_hidden_states.shape[0]
    context_len = context_rows * inner_count * outer_count
    projected_q = lax.psum_scatter(
        jnp.dot(query_states, w_query, preferred_element_type=jnp.float32),
        "inner",
        scatter_dimension=0,
        tiled=True,
    )
    row_first = outer_at * query_states.shape[0] + inner_at * query_rows
    query_pos = (context_len + (row_first + jnp.arange(query_rows)) % QWIN).astype(jnp.float32)
    queries = rotate(projected_q.reshape(query_rows, heads, HEAD_SIZE), query_pos).astype(
        jnp.bfloat16
    )
    queries = queries.reshape(query_rows, query_cols)
    query_tags = lax.dynamic_slice_in_dim(query_segments, inner_at * query_rows, query_rows, 0)
    hot = (query_tags[:, None] == jnp.arange(HEAD_SIZE)[None, :]).astype(jnp.bfloat16)
    kv_partial = jnp.dot(
        context_hidden_states,
        key_value_weight.reshape(key_value_weight.shape[0], -1),
        preferred_element_type=jnp.float32,
    )
    kv_partial = kv_partial.reshape(context_rows, key_value_weight.shape[1], 2 * HEAD_SIZE)
    kv_local = lax.psum_scatter(kv_partial, "head", scatter_dimension=1, tiled=True)
    key_first = (inner_at * outer_count + outer_at) * context_rows
    key_pos = (key_first + jnp.arange(context_rows)).astype(jnp.float32)
    keys = rotate(kv_local[:, :, :HEAD_SIZE], key_pos).astype(jnp.bfloat16)[:, 0]
    values = kv_local[:, 0, HEAD_SIZE:].astype(jnp.bfloat16)
    packed = jnp.concatenate([keys, values, penalties(key_segments, KBLK)], axis=-1)
    gathered = lax.all_gather(packed, "inner", axis=0, tiled=True)
    ka = jnp.concatenate([gathered[:, :HEAD_SIZE], gathered[:, 2 * HEAD_SIZE :]], axis=-1)
    va = jnp.concatenate(
        [gathered[:, HEAD_SIZE : 2 * HEAD_SIZE], jnp.ones((ka.shape[0], HEAD_SIZE), jnp.bfloat16)],
        axis=-1,
    )
    qall = lax.all_gather(jnp.concatenate([queries, hot], axis=-1), "outer", axis=0, tiled=True)
    part, lse = attention(qall[:, :query_cols], qall[:, query_cols:], ka, va, heads)
    lse = lse[:, :heads].reshape(outer_count, query_rows, heads)
    part = lax.all_to_all(
        part.reshape(outer_count, query_rows, query_cols), "outer", 0, 0, tiled=True
    )
    lse = lax.all_to_all(lse, "outer", 0, 0, tiled=True)
    weight = jnp.exp2(lse - jnp.max(lse, axis=0, keepdims=True))
    weight = weight / jnp.sum(weight, axis=0, keepdims=True)
    attended = jnp.sum(
        part.reshape(outer_count, query_rows, heads, HEAD_SIZE).astype(jnp.float32)
        * weight[..., None],
        axis=0,
    )
    attended = attended.reshape(query_rows, query_cols).astype(jnp.bfloat16)
    output_flat = w_output.reshape(w_output.shape[0], -1)
    terms = jnp.dot(
        lax.all_gather(attended, "inner", axis=0, tiled=True),
        output_flat,
        preferred_element_type=jnp.float32,
    )
    terms = terms.reshape(terms.shape[0], head_count, -1)
    mixed = lax.psum_scatter(
        terms.astype(jnp.bfloat16), "head", scatter_dimension=1, tiled=True
    ).astype(jnp.float32)
    return mixed.reshape(terms.shape[0], -1).astype(jnp.bfloat16)


def solution(mesh):
    in_specs = (
        P("outer", "inner"),
        P(("inner", "outer"), "head"),
        P(("inner", "outer")),
        P("outer"),
        P("inner", "head"),
        P("head", None, None),
        P("head", None, "inner"),
    )
    out_specs = P("outer", ("head", "inner"))
    return jax.shard_map(
        on_device, mesh=mesh, in_specs=in_specs, out_specs=out_specs, check_vma=False
    )
```
